32 devices in a mesh: layer: 2 (over y), lat: 4 (over x, core), tok: 4 (over z).
Axes of the slice: x: 2, y: 2, z: 4, core: 2. Of those that a mesh axis runs over, the one named last changes fastest.
Arguments:
- mlp_inputs: bfloat16 [2, 384, 4096], P('layer', ('lat', 'tok')), may hold values from -6 to 6
- mlp_outputs: bfloat16 [2, 384, 4096], P('layer', ('lat', 'tok')), may hold values from -6 to 6
- encoder: bfloat16 [2, 4096, 16384], P('layer', None, ('lat', 'tok')), may hold values from -0.09375 to 0.09375
- encoder_bias: float32 [2, 16384], P('layer', ('lat', 'tok')), may hold values from -3 to 3
- active_words: int32 [2, 384, 1024], P('layer', None, ('lat', 'tok')), may hold values from 0 to 65535
- decoder: bfloat16 [2, 16384, 4096], P('layer', ('lat', 'tok')), may hold values from -0.0234375 to 0.0234375
Outputs:
- reconstruction_error: bfloat16 [2, 384, 4096], P('layer', ('lat', 'tok'))
- decoder_grad: bfloat16 [2, 16384, 4096], P('layer', ('lat', 'tok'))
The draws below stay inside these ranges and needn't reach their ends.
Inputs may be any that keep to these rules, and one draw needn't show every extreme that they name: `active_words`: each word holds 16 independent gate decisions of one token in its low 16 bits.
All inputs are finite; a program needn't handle non-finite values.
Results may differ from the reference program's by a relative error of at most 0.0037.
Values may be sent and summed in bfloat16 or wider, within the bound.
A program may use at most 128 MiB of HBM per device.

```python
import jax
import jax.numpy as jnp

D = 4096
F = 16384
L = 2
TOKENS = 384


def plant(drawn, own_key, least, largest):
    index_at = [jax.random.randint(jax.random.fold_in(own_key, axis), (), 0, length) for axis, length in enumerate(drawn.shape)]
    main_axis = drawn.shape.index(max(drawn.shape))
    next_to = index_at[:main_axis] + [(index_at[main_axis] + 1) % drawn.shape[main_axis]] + index_at[main_axis + 1:]
    return drawn.at[tuple(index_at)].set(least).at[tuple(next_to)].set(largest)


def block_levels(key, extent, cuts, low, top_value):
    def one(position, shards_of):
        heights = jax.random.uniform(jax.random.fold_in(jax.random.fold_in(key, 6), position), (shards_of,), jnp.float32, low / len(cuts), top_value / len(cuts))
        return jnp.repeat(jnp.exp(heights), extent[position] // shards_of).reshape((-1,) + (1,) * (len(extent) - position - 1))

    factor_of = one(*cuts[0])
    for cut in cuts[1:]:
        factor_of = factor_of * one(*cut)
    return factor_of


def normal_values(rng, shape, spread, limit, pieces=(), held_as=jnp.bfloat16):
    result = spread * jax.random.normal(rng, shape, jnp.float32)
    if pieces:
        result = result * block_levels(rng, shape, pieces, -0.22, 0.18)
    return jnp.clip(result, -limit, limit).astype(held_as)


def setup_inputs(seed: int = 0) -> dict:
    splits = jax.random.split(jax.random.key(seed), 7)
    return {
        "mlp_inputs": normal_values(splits[0], (L, TOKENS, D), 1.0, 6.0, ((0, 2), (1, 16))),
        "mlp_outputs": normal_values(splits[1], (L, TOKENS, D), 1.0, 6.0, ((0, 2), (1, 16))),
        "encoder": normal_values(splits[2], (L, D, F), D ** -0.5, 0.09375, ((0, 2), (2, 16))),
        "encoder_bias": normal_values(splits[3], (L, F), 0.5, 3.0, ((0, 2), (1, 16)), jnp.float32),
        "active_words": plant(jax.random.randint(splits[4], (L, TOKENS, F // 16), 0, 65536), jax.random.fold_in(splits[4], 1), 0, 65535).astype(jnp.int32),
        "decoder": normal_values(splits[5], (L, F, D), (4 * F) ** -0.5, 0.0234375, ((0, 2), (1, 16))),
    }


def unpack_words(words):
    shifts = jnp.arange(16, dtype=jnp.int32)
    bits = jnp.right_shift(words[..., None], shifts) & 1
    return bits.reshape(words.shape[:-1] + (words.shape[-1] * 16,)).astype(jnp.float32)


def reference(mlp_inputs, mlp_outputs, encoder, encoder_bias, active_words, decoder):
    latents = []
    writes = []
    for layer in range(L):
        before_gate = jnp.dot(mlp_inputs[layer], encoder[layer], preferred_element_type=jnp.float32)
        before_gate = before_gate + encoder_bias[layer].astype(jnp.float32)[None, :]
        latent = (unpack_words(active_words[layer]) * before_gate).astype(jnp.bfloat16)
        latents.append(latent)
        writes.append(jnp.dot(latent, decoder[layer], preferred_element_type=jnp.float32))
    running = jnp.zeros((TOKENS, D), jnp.float32)
    differences = []
    for layer in range(L):
        running = running + writes[layer]
        differences.append(running - mlp_outputs[layer].astype(jnp.float32))
    later = jnp.zeros((TOKENS, D), jnp.float32)
    grads = [None] * L
    for layer in range(L - 1, -1, -1):
        later = later + differences[layer]
        signal = later.astype(jnp.bfloat16)
        total = jnp.dot(latents[layer].T, signal, preferred_element_type=jnp.float32)
        grads[layer] = (total / TOKENS).astype(jnp.bfloat16)
    return jnp.stack(differences).astype(jnp.bfloat16), jnp.stack(grads)
```

```python
import functools

import jax
import jax.numpy as jnp
from jax import lax
from jax.experimental import pallas as pl
from jax.experimental.pallas import tpu as pltpu
from jax.sharding import PartitionSpec as P

MESH = pl.DeviceIdType.MESH
CHUNKS = 4
TILE = 256
GRAD_TILE = 512


def kernel(sizes, x_ref, t_ref, enc_ref, bias_ref, words_ref, dec_ref,
           diff_ref, sig_ref, lat_ref,
           xg, sg, ss, enc, dec, acc, gate, latent, turned, w, r1, s2, p2, r2, s3, r3, w4, tg,
           x_sems, s_sems, rs_sems, tg_sems, loc_sems):
    L, A, T, r, C, cw, F = sizes
    H = A // 2
    N = A * T * r
    depth = T * r
    l, a, t = lax.axis_index("layer"), lax.axis_index("lat"), lax.axis_index("tok")
    h, lo = a // 2, lax.rem(a, 2)
    partner = h * 2 + 1 - lo
    started = []

    def mod(v, n):
        return lax.rem(v + n, n)

    def group(lat):
        return pl.ds(pl.multiple_of(lat * depth, 8), depth)

    def cols(c):
        return pl.ds(c * cw, cw)

    def remote(src, dst, sems, at, **where):
        return pltpu.make_async_remote_copy(
            src_ref=src, dst_ref=dst, send_sem=sems[0].at[at], recv_sem=sems[1].at[at],
            device_id=where, device_id_type=MESH)

    def send(src, dst, sems, at, when=None, **where):
        def make():
            return remote(src(), dst(), sems, at, **{k: v() for k, v in where.items()})

        def run(what):
            if when is None:
                what()
            else:
                pl.when(when())(what)

        run(lambda: make().start())
        started.append(lambda: run(lambda: make().wait_send()))

    def arrived(dst, sems, at, **where):
        remote(dst, dst, sems, at, **where).wait_recv()

    def local_copy(src, dst, at):
        return pltpu.make_async_copy(src, dst, loc_sems.at[at])

    class Gather:
        def __init__(self, buf, sems):
            self.buf, self.right, self.left, self.hi, self.lo = buf, sems[0:2], sems[2:4], sems[4:6], sems[6:8]

        def block(self, c, lat, tok):
            return self.buf.at[c, lat, tok]

        def across(self, c, src, tok, slot, when=None):
            for d in range(1, H):
                send(src, lambda: self.block(c, a, tok), self.hi, (c, d - 1, slot), when=when,
                     lat=lambda d=d: mod(h + d, H) * 2 + lo)

        def first(self, c, src):
            if T > 1:
                send(src, lambda: self.block(c, a, t), self.right, (c, 0), when=lambda: t < T - 1, tok=lambda: t + 1)
                send(src, lambda: self.block(c, a, t), self.left, (c, 0), when=lambda: t > 0, tok=lambda: t - 1)
            self.across(c, src, t, 0)

        def hop(self, c, e):
            from_left, from_right = t - e, t + e

            @pl.when(t >= e)
            def _():
                arrived(self.block(c, a, from_left), self.right, (c, e - 1), tok=t - 1)

            if e < T - 1:
                send(lambda: self.block(c, a, from_left), lambda: self.block(c, a, from_left), self.right, (c, e),
                     when=lambda: (t >= e) & (t < T - 1), tok=lambda: t + 1)
            self.across(c, lambda: self.block(c, a, from_left), from_left, e, when=lambda: t >= e)

            @pl.when(t + e < T)
            def _():
                arrived(self.block(c, a, from_right), self.left, (c, e - 1), tok=t + 1)

            if e < T - 1:
                send(lambda: self.block(c, a, from_right), lambda: self.block(c, a, from_right), self.left, (c, e),
                     when=lambda: (t + e < T) & (t > 0), tok=lambda: t - 1)
            self.across(c, lambda: self.block(c, a, from_right), from_right, T - 1 + e, when=lambda: t + e < T)

        def share(self, c, lat, slot):
            send(lambda: self.buf.at[c, lat], lambda: self.buf.at[c, lat], self.lo, (c, slot), lat=lambda: partner)

        def mine(self, c):
            self.share(c, a, 0)

        def third(self, c):
            for d in range(1, H):
                other = mod(h - d, H) * 2 + lo
                arrived(self.block(c, other, t), self.hi, (c, d - 1, 0), lat=other)
                for e in range(1, T):
                    @pl.when(t >= e)
                    def _():
                        arrived(self.block(c, other, t - e), self.hi, (c, d - 1, e), lat=other)

                    @pl.when(t + e < T)
                    def _():
                        arrived(self.block(c, other, t + e), self.hi, (c, d - 1, T - 1 + e), lat=other)
                self.share(c, other, d)

        def fourth(self, c):
            for d in range(H):
                arrived(self.buf.at[c, mod(h - d, H) * 2 + 1 - lo], self.lo, (c, d), lat=partner)

    gx, gs = Gather(xg, x_sems), Gather(sg, s_sems)
    rs_lo, rs_hi, rs_tok, rs_layer = rs_sems[0:2], rs_sems[2:4], rs_sems[4:6], rs_sems[6:8]

    enc_loads, dec_loads, own_loads = [], [], []
    for c in range(C):
        own_loads.append(local_copy(x_ref.at[0, :, cols(c)], xg.at[c, a, t], c))
        enc_loads.append(local_copy(enc_ref.at[0, cols(c), :], enc.at[c], C + c))
        dec_loads.append(local_copy(dec_ref.at[0, :, cols(c)], dec.at[c], 2 * C + c))
    own_target = local_copy(t_ref.at[0], tg.at[l], 3 * C)
    for copy in own_loads + enc_loads:
        copy.start()

    barrier = pltpu.get_barrier_semaphore()
    count = 0
    for name, index, n in (("tok", t, T), ("layer", l, L)):
        for d in range(1, n):
            pl.semaphore_signal(barrier, inc=1, device_id={name: mod(index + d, n)}, device_id_type=MESH)
            count += 1
    for d in range(1, H):
        pl.semaphore_signal(barrier, inc=1, device_id={"lat": mod(h + d, H) * 2 + lo}, device_id_type=MESH)
        count += 1
    pl.semaphore_signal(barrier, inc=1, device_id={"lat": partner}, device_id_type=MESH)
    pl.semaphore_wait(barrier, count + 1)

    for c in range(C):
        gx.first(c, lambda c=c: x_ref.at[0, :, cols(c)])
    for d in range(1, L):
        send(lambda: t_ref.at[0], lambda: tg.at[l], tg_sems, d - 1, layer=lambda d=d: mod(l + d, L))
    own_target.start()
    for copy in dec_loads:
        copy.start()

    W = words_ref.shape[1]
    words = words_ref[0]
    low = (words & 255).astype(jnp.float32).astype(jnp.bfloat16)
    high = (jnp.right_shift(words, 8) & 255).astype(jnp.float32).astype(jnp.bfloat16)

    @pl.loop(0, F // TILE)
    def _(n):
        at = pl.ds(pl.multiple_of(n * TILE, TILE), TILE)
        col = lax.broadcasted_iota(jnp.int32, (W, TILE), 1) + n * TILE
        row = lax.broadcasted_iota(jnp.int32, (W, TILE), 0)
        same = jnp.right_shift(col, 4) == row
        first_byte = (col & 8) == 0
        spread_low = jnp.where(same & first_byte, 1.0, 0.0).astype(jnp.bfloat16)
        spread_high = jnp.where(same & jnp.logical_not(first_byte), 1.0, 0.0).astype(jnp.bfloat16)
        byte = (lax.dot_general(low, spread_low, (((0,), (0,)), ((), ())), preferred_element_type=jnp.float32)
                + lax.dot_general(high, spread_high, (((0,), (0,)), ((), ())), preferred_element_type=jnp.float32)).astype(jnp.int32)
        shift = lax.broadcasted_iota(jnp.int32, byte.shape, 1) & 7
        gate[:, at] = (jnp.right_shift(byte, shift) & 1).astype(jnp.float32)

    def matmul_in(c):
        enc_loads[c].wait()

        @pl.loop(0, F // TILE)
        def _(n):
            at = pl.ds(pl.multiple_of(n * TILE, TILE), TILE)
            part = jnp.dot(xg[c].reshape(N, cw), enc[c, :, at], preferred_element_type=jnp.float32)
            if c > 0:
                part = acc[:, at] + part
            if c < C - 1:
                acc[:, at] = part
            else:
                latent[:, at] = (gate[:, at] * (part + bias_ref[:, at])).astype(jnp.bfloat16)

    for c in range(C):
        own_loads[c].wait()
    for e in range(1, T):
        for c in range(C):
            gx.hop(c, e)
            if e == T - 1:
                gx.mine(c)
    if T == 1:
        for c in range(C):
            gx.mine(c)
    for s in range(C + 1):
        if s < C:
            gx.third(s)
        if s >= 1:
            gx.fourth(s - 1)
            matmul_in(s - 1)

    def stage_matmul(c):
        dec_loads[c].wait()

        @pl.loop(0, cw // TILE)
        def _(n):
            at = pl.ds(pl.multiple_of(n * TILE, TILE), TILE)
            w[c, :, at] = jnp.dot(latent[...], dec[c, :, at], preferred_element_type=jnp.float32).astype(jnp.bfloat16)

        for k in range(H):
            to = mod(h + 1 + k, H)
            send(lambda to=to: w.at[c, group(to * 2 + 1 - lo), :], lambda to=to: r1.at[c, to], rs_lo, (c, k),
                 lat=lambda: partner)

    def stage_lo(c):
        for k in range(H):
            to = mod(h + 1 + k, H)
            arrived(r1.at[c, to], rs_lo, (c, k), lat=partner)
            total = w[c, group(to * 2 + lo), :].astype(jnp.float32) + r1[c, to].astype(jnp.float32)
            if k < H - 1:
                s2[c, k] = total.astype(jnp.bfloat16)
                send(lambda k=k: s2.at[c, k], lambda k=k: r2.at[c, k], rs_hi, (c, k), lat=lambda to=to: to * 2 + lo)
            else:
                p2[c] = total

    def stage_hi(c):
        total = p2[c]
        for k in range(H - 1):
            arrived(r2.at[c, k], rs_hi, (c, k), lat=mod(h - 1 - k, H) * 2 + lo)
            total = total + r2[c, k].astype(jnp.float32)
        total = total.astype(jnp.bfloat16).astype(jnp.float32)
        for i in range(T):
            s3[c, i] = total[i * r:(i + 1) * r].astype(jnp.bfloat16)
        for d in range(1, T):
            to = mod(t + d, T)
            send(lambda to=to: s3.at[c, to], lambda d=d: r3.at[c, d - 1], rs_tok, (c, d - 1), tok=lambda to=to: to)

    def stage_tok(c):
        total = s3[c, t].astype(jnp.float32)
        for d in range(1, T):
            arrived(r3.at[c, d - 1], rs_tok, (c, d - 1), tok=mod(t - d, T))
            total = total + r3[c, d - 1].astype(jnp.float32)
        w4[c, l] = total.astype(jnp.bfloat16)
        for d in range(1, L):
            send(lambda: w4.at[c, l], lambda: w4.at[c, l], rs_layer, (c, d - 1), layer=lambda d=d: mod(l + d, L))

    own_sig = []

    def stage_layer(c):
        if c == 0:
            own_target.wait()
            for d in range(1, L):
                arrived(tg.at[mod(l - d, L)], tg_sems, d - 1, layer=mod(l - d, L))
        for d in range(1, L):
            arrived(w4.at[c, mod(l - d, L)], rs_layer, (c, d - 1), layer=mod(l - d, L))
        running = jnp.zeros((r, cw), jnp.float32)
        later = jnp.zeros((r, cw), jnp.float32)
        mine = jnp.zeros((r, cw), jnp.float32)
        for i in range(L):
            running = running + w4[c, i].astype(jnp.float32)
            difference = running - tg[i, :, cols(c)].astype(jnp.float32)
            mine = mine + difference * (l == i).astype(jnp.float32)
            later = later + difference * (l <= i).astype(jnp.float32)
        diff_ref[:, cols(c)] = mine.astype(jnp.bfloat16)
        ss[c] = later.astype(jnp.bfloat16)
        gs.first(c, lambda: ss.at[c])
        copy = local_copy(ss.at[c], sg.at[c, a, t], 3 * C + 2 + c)
        copy.start()
        own_sig.append(copy)

    def stage_hop(e):
        def run(c):
            gs.hop(c, e)
        return run

    def stage_mine(c):
        own_sig[c].wait()
        gs.mine(c)

    outs = []

    def stage_out(c):
        gs.fourth(c)
        copy = local_copy(sg.at[c], sig_ref.at[:, :, :, cols(c)], 4 * C + 2 + c)
        copy.start()
        outs.append(copy)

    def turn():
        @pl.loop(0, F // TILE)
        def _(n):
            at = pl.ds(pl.multiple_of(n * TILE, TILE), TILE)
            turned[at, :] = latent[:, at].astype(jnp.float32).T.astype(jnp.bfloat16)

        copy = local_copy(turned, lat_ref, 3 * C + 1)
        copy.start()
        outs.append(copy)

    stages = (stage_matmul, stage_lo, stage_hi, stage_tok, stage_layer, *(stage_hop(e) for e in range(1, T)),
              stage_mine, gs.third, stage_out)
    for s in range(C + len(stages) - 1):
        for i, stage in enumerate(stages):
            if 0 <= s - i < C:
                stage(s - i)
        if s == C:
            turn()

    for copy in outs:
        copy.wait()
    for wait in started:
        wait()


def product(latent_ref, signal_ref, diff_ref, out_diff_ref, grad_ref):
    total = jnp.dot(latent_ref[...], signal_ref[...], preferred_element_type=jnp.float32)
    grad_ref[0] = (total * (1.0 / signal_ref.shape[0])).astype(jnp.bfloat16)
    out_diff_ref[0] = diff_ref[...]


def gradient(latent, signal, difference):
    F, N = latent.shape
    r, D = difference.shape
    wide = min(GRAD_TILE, D)
    return pl.pallas_call(
        product,
        grid=(D // wide,),
        in_specs=[pl.BlockSpec((F, N), lambda i: (0, 0)), pl.BlockSpec((N, wide), lambda i: (0, i)),
                  pl.BlockSpec((r, wide), lambda i: (0, i))],
        out_specs=(pl.BlockSpec((1, r, wide), lambda i: (0, 0, i)), pl.BlockSpec((1, F, wide), lambda i: (0, 0, i))),
        out_shape=(jax.ShapeDtypeStruct((1, r, D), jnp.bfloat16), jax.ShapeDtypeStruct((1, F, D), jnp.bfloat16)),
        compiler_params=pltpu.CompilerParams(vmem_limit_bytes=40 * 1024 * 1024),
    )(latent, signal, difference)


def fused(mesh, mlp_inputs, mlp_outputs, encoder, encoder_bias, active_words, decoder):
    L, A, T = mesh.shape["layer"], mesh.shape["lat"], mesh.shape["tok"]
    _, r, D = mlp_inputs.shape
    F = encoder.shape[2]
    N = active_words.shape[1]
    C, H, depth = CHUNKS, A // 2, T * r
    cw = D // C
    bf, f32 = jnp.bfloat16, jnp.float32
    dma = pltpu.SemaphoreType.DMA
    hbm = pl.BlockSpec(memory_space=pl.ANY)
    vmem = pl.BlockSpec(memory_space=pltpu.VMEM)

    def pair(*shape):
        return [dma(tuple(max(n, 1) for n in shape))] * 2

    gather = pair(C, T - 1) + pair(C, T - 1) + pair(C, H - 1, 2 * T - 1) + pair(C, H)
    return pl.pallas_call(
        functools.partial(kernel, (L, A, T, r, C, cw, F)),
        out_shape=(jax.ShapeDtypeStruct((r, D), bf), jax.ShapeDtypeStruct((A, T, r, D), bf), jax.ShapeDtypeStruct((F, N), bf)),
        in_specs=[hbm, hbm, hbm, vmem, vmem, hbm],
        out_specs=(vmem, hbm, hbm),
        scratch_shapes=[
            pltpu.VMEM((C, A, T, r, cw), bf),
            pltpu.VMEM((C, A, T, r, cw), bf),
            pltpu.VMEM((C, r, cw), bf),
            pltpu.VMEM((C, cw, F), bf),
            pltpu.VMEM((C, F, cw), bf),
            pltpu.VMEM((N, F), f32),
            pltpu.VMEM((N, F), f32),
            pltpu.VMEM((N, F), bf),
            pltpu.VMEM((F, N), bf),
            pltpu.VMEM((C, N, cw), bf),
            pltpu.VMEM((C, H, depth, cw), bf),
            pltpu.VMEM((C, max(H - 1, 1), depth, cw), bf),
            pltpu.VMEM((C, depth, cw), f32),
            pltpu.VMEM((C, max(H - 1, 1), depth, cw), bf),
            pltpu.VMEM((C, T, r, cw), bf),
            pltpu.VMEM((C, T - 1, r, cw), bf),
            pltpu.VMEM((C, L, r, cw), bf),
            pltpu.VMEM((L, r, D), bf),
            gather,
            gather,
            pair(C, H) + pair(C, H - 1) + pair(C, T - 1) + pair(C, L - 1),
            pair(L - 1),
            dma((5 * C + 2,)),
        ],
        compiler_params=pltpu.CompilerParams(
            collective_id=0, has_side_effects=True, vmem_limit_bytes=60 * 1024 * 1024),
    )(mlp_inputs, mlp_outputs, encoder, encoder_bias, jnp.transpose(active_words, (0, 2, 1)), decoder)


def local(mesh, mlp_inputs, mlp_outputs, encoder, encoder_bias, active_words, decoder):
    difference, signal, latent = fused(mesh, mlp_inputs, mlp_outputs, encoder, encoder_bias, active_words, decoder)
    return gradient(latent, signal.reshape(latent.shape[1], signal.shape[-1]), difference)


def solution(mesh):
    in_specs = (
        P("layer", ("lat", "tok"), None),
        P("layer", ("lat", "tok"), None),
        P("layer", None, ("lat", "tok")),
        P("layer", ("lat", "tok")),
        P("layer", None, ("lat", "tok")),
        P("layer", ("lat", "tok"), None),
    )
    out_specs = (P("layer", ("lat", "tok"), None), P("layer", ("lat", "tok"), None))
    return jax.shard_map(functools.partial(local, mesh), mesh=mesh, in_specs=in_specs, out_specs=out_specs, check_vma=False)
```

```python
import functools

import jax
import jax.numpy as jnp
from jax import lax
from jax.experimental import pallas as pl
from jax.experimental.pallas import tpu as pltpu
from jax.sharding import PartitionSpec as P

MESH = pl.DeviceIdType.MESH
IN_CHUNKS = 4
CHUNKS = 8
AHEAD_IN = ()
AHEAD = ()
TILE = 512
IN_PACE = 4.3
PACE = 10.0
MXU = 6.0
HOP = 3.0
LINK = 2.8
STRAIGHT = 4
STRAIGHT_SUMS = 0


def kernel(sizes, x_ref, t_ref, enc_ref, bias_ref, words_ref, dec_ref,
           diff_ref, sig_ref, lat_ref,
           xg, sg, enc, dec, acc, gate, latent, turned, w, r1, s2, p2, r2, s3, r3, w4, tg, words_v, bias_v, diff_v,
           gather_recv, x_send, s_send, rs_send, rs_recv, tg_send, tg_recv, loc_sems):
    L, A, T, r, B, C, F = sizes
    D = x_ref.shape[2]
    bw, cw = D // B, D // C
    H = A // 2
    N = A * T * r
    depth = T * r
    l, a, t = lax.axis_index("layer"), lax.axis_index("lat"), lax.axis_index("tok")
    h, lo = a // 2, lax.rem(a, 2)
    partner = h * 2 + 1 - lo

    def mod(v, n):
        return lax.rem(v + n, n)

    def group(lat):
        return pl.ds(pl.multiple_of(lat * depth, 8), depth)

    def cols(c, wide=cw):
        return pl.ds(c * wide, wide)

    def remote(src, dst, send_sem, recv_sem, **where):
        return pltpu.make_async_remote_copy(
            src_ref=src, dst_ref=dst, send_sem=send_sem, recv_sem=recv_sem, device_id=where, device_id_type=MESH)

    def arrived(dst, sem, **where):
        remote(dst, dst, sem, sem, **where).wait_recv()

    def sent(ref, sem, **where):
        remote(ref, ref, sem, sem, **where).wait_send()

    def local_copy(src, dst, at):
        return pltpu.make_async_copy(src, dst, loc_sems.at[at])

    class Gather:
        def __init__(self, buf, sends, ahead, straight, count):
            self.straight = straight
            self.buf, self.ahead, self.count = buf, [c for c in ahead if c < count and H > 1], count
            self.chain, self.others, self.hi, self.lo = gather_recv
            self.sends = sends

        def block(self, c, lat, tok):
            return self.buf.at[c, lat, tok]

        def kind(self, c):
            return 1 if c in self.ahead else 0

        def other(self, d):
            return mod(h - d, H) * 2 + lo

        def chain_sem(self, c, d, tok):
            return self.chain.at[c, tok] if d == 0 else self.others.at[self.ahead.index(c), d - 1, tok]

        def move(self, src, dst, send_sem, recv_sem, **where):
            remote(src, dst, send_sem, recv_sem, **where).start()

        def along(self, c, d, src=None):
            lat = a if d == 0 else self.other(d)
            block = self.block(c, lat, t)

            @pl.when(t < T - 1)
            def _():
                self.move(src or block, block, self.sends.at[2 * self.kind(c)], self.chain_sem(c, d, t), tok=t + 1)

            @pl.when(t > 0)
            def _():
                self.move(src or block, block, self.sends.at[2 * self.kind(c) + 1], self.chain_sem(c, d, t), tok=t - 1)

        def across(self, c, tok, src=None):
            block = self.block(c, a, tok)
            for d in range(1, H):
                self.move(src or block, block, self.sends.at[4 + self.kind(c)], self.hi.at[c, d - 1, tok], lat=mod(h + d, H) * 2 + lo)

        def first(self, c, src=None):
            if c in self.ahead:
                self.across(c, t, src)
                self.along(c, 0, src)
            elif c in self.straight:
                block = self.block(c, a, t)
                for e in range(T - 1, 0, -1):
                    for fits, to in ((t + e < T, t + e), (t >= e, t - e)):
                        @pl.when(fits)
                        def _():
                            self.move(src or block, block, self.sends.at[7], self.chain_sem(c, 0, t), tok=to)
                self.across(c, t, src)
            else:
                self.along(c, 0, src)
                self.across(c, t, src)

        def cross(self, c):
            for d in range(1, H):
                arrived(self.block(c, self.other(d), t), self.hi.at[c, d - 1, t], lat=self.other(d))
                self.along(c, d)

        def hop(self, c, e):
            for d in range(H if c in self.ahead else 1):
                lat = a if d == 0 else self.other(d)
                for here, tok, source, onward, end, way in (
                        (t >= e, t - e, t - 1, t + 1, t < T - 1, 0), (t + e < T, t + e, t + 1, t - 1, t > 0, 1)):
                    @pl.when(here)
                    def _():
                        block = self.block(c, lat, tok)
                        arrived(block, self.chain_sem(c, d, tok), tok=tok if c in self.straight else source)
                        if e < T - 1 and c not in self.straight:
                            @pl.when(end)
                            def _():
                                self.move(block, block, self.sends.at[2 * self.kind(c) + way], self.chain_sem(c, d, tok), tok=onward)
                        if c not in self.ahead:
                            self.across(c, tok)

        def share(self, c, lat, slot):
            group = self.buf.at[c, lat]
            self.move(group, group, self.sends.at[6], self.lo.at[c, slot], lat=partner)

        def mine(self, c):
            self.share(c, a, 0)
            if c in self.ahead:
                for d in range(1, H):
                    self.share(c, self.other(d), d)

        def third(self, c):
            if c not in self.ahead:
                for d in range(1, H):
                    for tok in range(T):
                        arrived(self.block(c, self.other(d), tok), self.hi.at[c, d - 1, tok], lat=self.other(d))
                    self.share(c, self.other(d), d)

        def fourth(self, c):
            for d in range(H):
                arrived(self.buf.at[c, mod(h - d, H) * 2 + 1 - lo], self.lo.at[c, d], lat=partner)

        def finish(self):
            ahead, straight = len(self.ahead), len(self.straight)
            if straight and T > 1:
                sent(self.buf.at[pl.ds(0, straight), 0, pl.ds(0, T - 1)], self.sends.at[7], lat=partner)
                if H > 1:
                    sent(self.buf.at[pl.ds(0, straight), pl.ds(0, H - 1)], self.sends.at[4], lat=self.other(1))
            for kind, n, wide in ((0, self.count - ahead - straight, 1), (1, ahead, H)):
                if n == 0:
                    continue
                for m in range(1, T):
                    blocks = self.buf.at[pl.ds(0, n), pl.ds(0, wide), pl.ds(0, m)]

                    @pl.when(t + 1 == m)
                    def _():
                        sent(blocks, self.sends.at[2 * kind], tok=t + 1)

                    @pl.when(T - t == m)
                    def _():
                        sent(blocks, self.sends.at[2 * kind + 1], tok=t - 1)
                if H > 1:
                    sent(self.buf.at[pl.ds(0, n), pl.ds(0, H - 1), pl.ds(0, 1 if kind else T)], self.sends.at[4 + kind],
                         lat=self.other(1))
            sent(self.buf.at[:, pl.ds(0, H)], self.sends.at[6], lat=partner)

    straight = [c for c in range(C) if c >= C - STRAIGHT]
    gx, gs = Gather(xg, x_send, AHEAD_IN, [], B), Gather(sg, s_send, AHEAD, straight, C)
    recv_lo, recv_hi, recv_tok, recv_layer = rs_recv

    words_in = local_copy(words_ref.at[0], words_v, 2 * B + C)
    bias_in = local_copy(bias_ref, bias_v, 2 * B + C + 1)
    words_in.start()
    bias_in.start()
    enc_loads, dec_loads, own_loads = [], [], []
    for c in range(B):
        own_loads.append(local_copy(x_ref.at[0, :, cols(c, bw)], xg.at[c, a, t], c))
        enc_loads.append(local_copy(enc_ref.at[0, cols(c, bw), :], enc.at[c], B + c))
    for c in range(C):
        dec_loads.append(local_copy(dec_ref.at[0, :, cols(c)], dec.at[c], 2 * B + c))
    own_target = local_copy(t_ref.at[0], tg.at[l], 2 * B + C + 2)
    for copy in own_loads + enc_loads:
        copy.start()

    barrier = pltpu.get_barrier_semaphore()
    count = 0
    for name, index, n in (("tok", t, T), ("layer", l, L)):
        for d in range(1, n):
            pl.semaphore_signal(barrier, inc=1, device_id={name: mod(index + d, n)}, device_id_type=MESH)
            count += 1
    for d in range(1, H):
        pl.semaphore_signal(barrier, inc=1, device_id={"lat": mod(h + d, H) * 2 + lo}, device_id_type=MESH)
        count += 1
    pl.semaphore_signal(barrier, inc=1, device_id={"lat": partner}, device_id_type=MESH)
    pl.semaphore_wait(barrier, count + 1)

    for c in range(B):
        gx.first(c, x_ref.at[0, :, cols(c, bw)])
    for d in range(1, L):
        remote(t_ref.at[0], tg.at[l], tg_send, tg_recv.at[d - 1], layer=mod(l + d, L)).start()
    own_target.start()
    for copy in dec_loads:
        copy.start()

    W = words_v.shape[0]
    words_in.wait()
    bias_in.wait()
    words = words_v[...]
    low = (words & 255).astype(jnp.float32).astype(jnp.bfloat16)
    high = (jnp.right_shift(words, 8) & 255).astype(jnp.float32).astype(jnp.bfloat16)

    @pl.loop(0, F // TILE)
    def _(n):
        at = pl.ds(pl.multiple_of(n * TILE, TILE), TILE)
        col = lax.broadcasted_iota(jnp.int32, (W, TILE), 1) + n * TILE
        row = lax.broadcasted_iota(jnp.int32, (W, TILE), 0)
        same = jnp.right_shift(col, 4) == row
        first_byte = (col & 8) == 0
        spread_low = jnp.where(same & first_byte, 1.0, 0.0).astype(jnp.bfloat16)
        spread_high = jnp.where(same & jnp.logical_not(first_byte), 1.0, 0.0).astype(jnp.bfloat16)
        byte = (lax.dot_general(low, spread_low, (((0,), (0,)), ((), ())), preferred_element_type=jnp.float32)
                + lax.dot_general(high, spread_high, (((0,), (0,)), ((), ())), preferred_element_type=jnp.float32)).astype(jnp.int32)
        shift = lax.broadcasted_iota(jnp.int32, byte.shape, 1) & 7
        gate[:, at] = (jnp.right_shift(byte, shift) & 1).astype(jnp.float32)

    def matmul_in(c):
        enc_loads[c].wait()

        @pl.loop(0, F // TILE)
        def _(n):
            at = pl.ds(pl.multiple_of(n * TILE, TILE), TILE)
            part = jnp.dot(xg[c].reshape(N, bw), enc[c, :, at], preferred_element_type=jnp.float32)
            if c > 0:
                part = acc[:, at] + part
            if c < B - 1:
                acc[:, at] = part
            else:
                latent[:, at] = (gate[:, at] * (part + bias_v[:, at])).astype(jnp.bfloat16)

    for c in range(B):
        own_loads[c].wait()
    for c in gx.ahead:
        gx.cross(c)
    def hop_in(e):
        return lambda c: gx.hop(c, e)

    def last_in(c):
        gx.fourth(c)
        matmul_in(c)

    block = IN_PACE / B
    arrivals = [(hop_in(e), IN_PACE * e) for e in range(1, T)]
    arrivals += [(gx.mine, IN_PACE * (T - 1)), (gx.third, IN_PACE * (T - 1) + 2.6), (last_in, IN_PACE * (T - 1) + 4.2)]
    for _, i, c in sorted((begin + c * block, i, c) for i, (_, begin) in enumerate(arrivals) for c in range(B)):
        arrivals[i][0](c)

    def stage_matmul(c):
        dec_loads[c].wait()

        @pl.loop(0, cw // TILE)
        def _(n):
            at = pl.ds(pl.multiple_of(n * TILE, TILE), TILE)
            w[c, :, at] = jnp.dot(latent[...], dec[c, :, at], preferred_element_type=jnp.float32).astype(jnp.bfloat16)

        for k in range(H):
            to = mod(h + 1 + k, H)
            remote(w.at[c, group(to * 2 + 1 - lo), :], r1.at[c, to], rs_send.at[0], recv_lo.at[c, k], lat=partner).start()

    def stage_lo(c):
        for k in range(H):
            to = mod(h + 1 + k, H)
            arrived(r1.at[c, to], recv_lo.at[c, k], lat=partner)
            total = w[c, group(to * 2 + lo), :].astype(jnp.float32) + r1[c, to].astype(jnp.float32)
            if k < H - 1:
                s2[c, k] = total.astype(jnp.bfloat16)
                remote(s2.at[c, k], r2.at[c, k], rs_send.at[1], recv_hi.at[c, k], lat=to * 2 + lo).start()
            else:
                p2[c] = total

    def add_on(c, j, slot, source):
        arrived(r3.at[c, slot], recv_tok.at[c, slot], tok=source)
        p2[c, j * r:(j + 1) * r] = p2[c, j * r:(j + 1) * r] + r3[c, slot].astype(jnp.float32)

    def pass_on(c, j, to, slot):
        s3[c, j] = p2[c, j * r:(j + 1) * r].astype(jnp.bfloat16)
        remote(s3.at[c, j], r3.at[c, slot], rs_send.at[2], recv_tok.at[c, slot], tok=to).start()

    def stage_hi(c):
        total = p2[c]
        for k in range(H - 1):
            arrived(r2.at[c, k], recv_hi.at[c, k], lat=mod(h - 1 - k, H) * 2 + lo)
            total = total + r2[c, k].astype(jnp.float32)
        p2[c] = total
        if c >= C - STRAIGHT_SUMS:
            for j in range(T):
                s3[c, j] = total[j * r:(j + 1) * r].astype(jnp.bfloat16)
            for d in range(T - 1, 0, -1):
                to = mod(t + d, T)
                remote(s3.at[c, to], r3.at[c, t], rs_send.at[2], recv_tok.at[c, t], tok=to).start()
        elif T > 1:
            chain(0)(c)

    def chain(e):
        def run(c):
            @pl.when(t == e)
            def _():
                for j in range(T - 1, e, -1):
                    if e > 0:
                        add_on(c, j, j, e - 1)
                    pass_on(c, j, e + 1, j)
                if e > 0:
                    add_on(c, e, e, e - 1)

            @pl.when(t == T - 1 - e)
            def _():
                q = T - 1 - e
                for j in range(q):
                    if e > 0:
                        add_on(c, j, j, q + 1)
                    pass_on(c, j, q - 1, T if j == q - 1 else j)
                if e > 0:
                    add_on(c, q, T, q + 1)
        return run

    def stage_tok(c):
        total = p2[c, pl.ds(pl.multiple_of(t * r, 8), r)]
        if c >= C - STRAIGHT_SUMS:
            for d in range(1, T):
                source = mod(t - d, T)
                arrived(r3.at[c, source], recv_tok.at[c, source], tok=source)
                total = total + r3[c, source].astype(jnp.float32)
        w4[c, l] = total.astype(jnp.bfloat16)
        for d in range(1, L):
            remote(w4.at[c, l], w4.at[c, l], rs_send.at[3], recv_layer.at[c, d - 1], layer=mod(l + d, L)).start()

    diff_out = local_copy(diff_v, diff_ref, 2 * B + C + 3)

    def stage_layer(c):
        if c == 0:
            own_target.wait()
            for d in range(1, L):
                arrived(tg.at[mod(l - d, L)], tg_recv.at[d - 1], layer=mod(l - d, L))
        for d in range(1, L):
            arrived(w4.at[c, mod(l - d, L)], recv_layer.at[c, d - 1], layer=mod(l - d, L))
        running = jnp.zeros((r, cw), jnp.float32)
        later = jnp.zeros((r, cw), jnp.float32)
        mine = jnp.zeros((r, cw), jnp.float32)
        for i in range(L):
            running = running + w4[c, i].astype(jnp.float32)
            difference = running - tg[i, :, cols(c)].astype(jnp.float32)
            mine = mine + difference * (l == i).astype(jnp.float32)
            later = later + difference * (l <= i).astype(jnp.float32)
        sg[c, a, t] = later.astype(jnp.bfloat16)
        gs.first(c)
        diff_v[:, cols(c)] = mine.astype(jnp.bfloat16)
        if c == C - 1:
            diff_out.start()

    def stage_cross(c):
        if c in gs.ahead:
            gs.cross(c)

    def stage_hop(e):
        def run(c):
            gs.hop(c, e)
        return run

    def stage_out(c):
        gs.fourth(c)
        local_copy(sg.at[c], sig_ref.at[c], 2 * B + C + 4).start()

    lat_out = local_copy(turned, lat_ref, 2 * B + C + 5)

    def turn():
        @pl.loop(0, F // TILE)
        def _(n):
            at = pl.ds(pl.multiple_of(n * TILE, TILE), TILE)
            turned[at, :] = latent[:, at].astype(jnp.float32).T.astype(jnp.bfloat16)

        lat_out.start()

    pace = PACE / C
    plan = []
    for c in range(C):
        near, far = c >= C - STRAIGHT_SUMS, c in straight
        plan += [(c * MXU / C, stage_matmul, c), ((c + 1) * MXU / C + 0.5, stage_lo, c)]
        at = 4.0 + pace * (c + 1)
        plan += [(at, stage_hi, c)]
        if not near:
            plan += [(at + LINK * e, chain(e), c) for e in range(1, T)]
        at += 4.0 if near else LINK * (T - 1) + 0.2
        plan += [(at, stage_tok, c), (at + 2.5, stage_layer, c), (at + 5.0, stage_cross, c)]
        plan += [(at + (4.5 + 0.5 * e if far else 2.5 + HOP * e), stage_hop(e), c) for e in range(1, T)]
        at += 4.5 + 0.5 * (T - 1) if far else 2.5 + HOP * (T - 1)
        plan += [(at, gs.mine, c), (at + 2.5, gs.third, c), (at + 4.0, stage_out, c)]
    turned_yet = False
    for when, stage, c in sorted(plan, key=lambda p: p[0]):
        if when > MXU + 2.0 and not turned_yet:
            turn()
            turned_yet = True
        stage(c)

    local_copy(sg, sig_ref, 2 * B + C + 4).wait()
    diff_out.wait()
    lat_out.wait()
    gx.finish()
    gs.finish()
    sent(r1, rs_send.at[0], lat=partner)
    if H > 1:
        sent(r2, rs_send.at[1], lat=gs.other(1))
    if T > 1:
        sent(s3.at[:, pl.ds(0, T - 1)], rs_send.at[2], tok=mod(t + 1, T))
    if L > 1:
        sent(w4.at[:, pl.ds(0, L - 1)], rs_send.at[3], layer=mod(l + 1, L))
        sent(tg.at[pl.ds(0, L - 1)], tg_send, layer=mod(l + 1, L))


def product(lat_ref, sig_ref, diff_ref, out_diff_ref, grad_ref, lat, sig, diff, grad, in_sems, out_sems):
    C, N, cw = sig_ref.shape
    loads = [pltpu.make_async_copy(sig_ref.at[c], sig.at[c], in_sems.at[c]) for c in range(C)]
    lat_in = pltpu.make_async_copy(lat_ref, lat, in_sems.at[C])
    diff_in = pltpu.make_async_copy(diff_ref, diff, in_sems.at[C + 1])
    outs = [pltpu.make_async_copy(grad.at[c], grad_ref.at[0, :, pl.ds(c * cw, cw)], out_sems.at[c]) for c in range(C)]
    outs.append(pltpu.make_async_copy(diff, out_diff_ref.at[0], out_sems.at[C]))
    for copy in (lat_in, *loads, diff_in):
        copy.start()
    lat_in.wait()
    for c in range(C):
        loads[c].wait()
        for n in range(0, cw, TILE):
            total = jnp.dot(lat[...], sig[c, :, n:n + TILE], preferred_element_type=jnp.float32)
            grad[c, :, n:n + TILE] = (total * (1.0 / N)).astype(jnp.bfloat16)
        outs[c].start()
    diff_in.wait()
    outs[C].start()
    for copy in outs:
        copy.wait()


def gradient(latent, signal, difference):
    F, N = latent.shape
    C, _, cw = signal.shape
    r, D = difference.shape
    bf = jnp.bfloat16
    hbm = pl.BlockSpec(memory_space=pl.ANY)
    return pl.pallas_call(
        product,
        in_specs=[hbm, hbm, hbm],
        out_specs=(hbm, hbm),
        out_shape=(jax.ShapeDtypeStruct((1, r, D), bf), jax.ShapeDtypeStruct((1, F, D), bf)),
        scratch_shapes=[
            pltpu.VMEM((F, N), bf),
            pltpu.VMEM((C, N, cw), bf),
            pltpu.VMEM((r, D), bf),
            pltpu.VMEM((C, F, cw), bf),
            pltpu.SemaphoreType.DMA((C + 2,)),
            pltpu.SemaphoreType.DMA((C + 1,)),
        ],
        compiler_params=pltpu.CompilerParams(vmem_limit_bytes=60 * 1024 * 1024),
    )(latent, signal, difference)


def fused(mesh, mlp_inputs, mlp_outputs, encoder, encoder_bias, active_words, decoder):
    L, A, T = mesh.shape["layer"], mesh.shape["lat"], mesh.shape["tok"]
    _, r, D = mlp_inputs.shape
    F = encoder.shape[2]
    N, W = active_words.shape[1:]
    B, C, H, depth = IN_CHUNKS, CHUNKS, A // 2, T * r
    bw, cw, most = D // B, D // C, max(IN_CHUNKS, CHUNKS)
    bf, f32 = jnp.bfloat16, jnp.float32
    hbm = pl.BlockSpec(memory_space=pl.ANY)

    def dma(*shape):
        return pltpu.SemaphoreType.DMA(tuple(max(n, 1) for n in shape))

    return pl.pallas_call(
        functools.partial(kernel, (L, A, T, r, B, C, F)),
        out_shape=(jax.ShapeDtypeStruct((r, D), bf), jax.ShapeDtypeStruct((C, A, T, r, cw), bf), jax.ShapeDtypeStruct((F, N), bf)),
        in_specs=[hbm] * 6,
        out_specs=(hbm, hbm, hbm),
        scratch_shapes=[
            pltpu.VMEM((B, A, T, r, bw), bf),
            pltpu.VMEM((C, A, T, r, cw), bf),
            pltpu.VMEM((B, bw, F), bf),
            pltpu.VMEM((C, F, cw), bf),
            pltpu.VMEM((N, F), f32),
            pltpu.VMEM((N, F), f32),
            pltpu.VMEM((N, F), bf),
            pltpu.VMEM((F, N), bf),
            pltpu.VMEM((C, N, cw), bf),
            pltpu.VMEM((C, H, depth, cw), bf),
            pltpu.VMEM((C, max(H - 1, 1), depth, cw), bf),
            pltpu.VMEM((C, depth, cw), f32),
            pltpu.VMEM((C, max(H - 1, 1), depth, cw), bf),
            pltpu.VMEM((C, T, r, cw), bf),
            pltpu.VMEM((C, T + 1, r, cw), bf),
            pltpu.VMEM((C, L, r, cw), bf),
            pltpu.VMEM((L, r, D), bf),
            pltpu.VMEM((W, N), jnp.int32),
            pltpu.VMEM((1, F), f32),
            pltpu.VMEM((r, D), bf),
            [dma(most, T), dma(max(len(AHEAD_IN), len(AHEAD)), H - 1, T), dma(most, H - 1, T), dma(most, H)],
            dma(8),
            dma(8),
            dma(4),
            [dma(C, H), dma(C, H - 1), dma(C, T + 1), dma(C, L - 1)],
            pltpu.SemaphoreType.DMA,
            dma(L - 1),
            dma(2 * B + C + 6),
        ],
        compiler_params=pltpu.CompilerParams(
            collective_id=0, has_side_effects=True, vmem_limit_bytes=60 * 1024 * 1024),
    )(mlp_inputs, mlp_outputs, encoder, encoder_bias, jnp.transpose(active_words, (0, 2, 1)), decoder)


def local(mesh, mlp_inputs, mlp_outputs, encoder, encoder_bias, active_words, decoder):
    difference, signal, latent = fused(mesh, mlp_inputs, mlp_outputs, encoder, encoder_bias, active_words, decoder)
    return gradient(latent, signal.reshape(signal.shape[0], latent.shape[1], signal.shape[-1]), difference)


def solution(mesh):
    in_specs = (
        P("layer", ("lat", "tok"), None),
        P("layer", ("lat", "tok"), None),
        P("layer", None, ("lat", "tok")),
        P("layer", ("lat", "tok")),
        P("layer", None, ("lat", "tok")),
        P("layer", ("lat", "tok"), None),
    )
    out_specs = (P("layer", ("lat", "tok"), None), P("layer", ("lat", "tok"), None))
    return jax.shard_map(functools.partial(local, mesh), mesh=mesh, in_specs=in_specs, out_specs=out_specs, check_vma=False)
```

```python
import functools

import jax
import jax.numpy as jnp
from jax import lax
from jax.experimental import pallas as pl
from jax.experimental.pallas import tpu as pltpu
from jax.sharding import PartitionSpec as P

MESH = pl.DeviceIdType.MESH
IN_CHUNKS = 4
CHUNKS = 8
AHEAD_IN = ()
AHEAD = ()
TILE = 512
IN_PACE = 4.3
PACE = 11.0
MXU = 6.0
HOP = 3.0
LINK = 2.3
HEAD = 4.0
NEXT = 2.5
IN_LAG = 2.6
IN_LAST = 4.2
STRAIGHT = 4
STRAIGHT_SUMS = 0


def kernel(sizes, x_ref, t_ref, enc_ref, bias_ref, words_ref, dec_ref,
           diff_ref, sig_ref, lat_ref,
           xg, sg, enc, dec, acc, gate, latent, turned, w, r1, s2, p2, r2, s3, r3, w4, tg, words_v, bias_v, diff_v,
           gather_recv, x_send, s_send, rs_send, rs_recv, tg_send, tg_recv, loc_sems):
    L, A, T, r, B, C, F = sizes
    D = x_ref.shape[2]
    bw, cw = D // B, D // C
    H = A // 2
    N = A * T * r
    depth = T * r
    l, a, t = lax.axis_index("layer"), lax.axis_index("lat"), lax.axis_index("tok")
    h, lo = a // 2, lax.rem(a, 2)
    partner = h * 2 + 1 - lo

    def mod(v, n):
        return lax.rem(v + n, n)

    def group(lat):
        return pl.ds(pl.multiple_of(lat * depth, 8), depth)

    def cols(c, wide=cw):
        return pl.ds(c * wide, wide)

    def remote(src, dst, send_sem, recv_sem, **where):
        return pltpu.make_async_remote_copy(
            src_ref=src, dst_ref=dst, send_sem=send_sem, recv_sem=recv_sem, device_id=where, device_id_type=MESH)

    def arrived(dst, sem, **where):
        remote(dst, dst, sem, sem, **where).wait_recv()

    def sent(ref, sem, **where):
        remote(ref, ref, sem, sem, **where).wait_send()

    def local_copy(src, dst, at):
        return pltpu.make_async_copy(src, dst, loc_sems.at[at])

    class Gather:
        def __init__(self, buf, sends, ahead, straight, count):
            self.straight = straight
            self.buf, self.ahead, self.count = buf, [c for c in ahead if c < count and H > 1], count
            self.chain, self.others, self.hi, self.lo = gather_recv
            self.sends = sends

        def block(self, c, lat, tok):
            return self.buf.at[c, lat, tok]

        def kind(self, c):
            return 1 if c in self.ahead else 0

        def other(self, d):
            return mod(h - d, H) * 2 + lo

        def chain_sem(self, c, d, tok):
            return self.chain.at[c, tok] if d == 0 else self.others.at[self.ahead.index(c), d - 1, tok]

        def move(self, src, dst, send_sem, recv_sem, **where):
            remote(src, dst, send_sem, recv_sem, **where).start()

        def along(self, c, d, src=None):
            lat = a if d == 0 else self.other(d)
            block = self.block(c, lat, t)

            @pl.when(t < T - 1)
            def _():
                self.move(src or block, block, self.sends.at[2 * self.kind(c)], self.chain_sem(c, d, t), tok=t + 1)

            @pl.when(t > 0)
            def _():
                self.move(src or block, block, self.sends.at[2 * self.kind(c) + 1], self.chain_sem(c, d, t), tok=t - 1)

        def across(self, c, tok, src=None):
            block = self.block(c, a, tok)
            for d in range(1, H):
                self.move(src or block, block, self.sends.at[4 + self.kind(c)], self.hi.at[c, d - 1, tok], lat=mod(h + d, H) * 2 + lo)

        def first(self, c, src=None):
            if c in self.ahead:
                self.across(c, t, src)
                self.along(c, 0, src)
            elif c in self.straight:
                block = self.block(c, a, t)
                for e in range(T - 1, 0, -1):
                    for fits, to in ((t + e < T, t + e), (t >= e, t - e)):
                        @pl.when(fits)
                        def _():
                            self.move(src or block, block, self.sends.at[7], self.chain_sem(c, 0, t), tok=to)
                self.across(c, t, src)
            else:
                self.along(c, 0, src)
                self.across(c, t, src)

        def cross(self, c):
            for d in range(1, H):
                arrived(self.block(c, self.other(d), t), self.hi.at[c, d - 1, t], lat=self.other(d))
                self.along(c, d)

        def hop(self, c, e):
            for d in range(H if c in self.ahead else 1):
                lat = a if d == 0 else self.other(d)
                for here, tok, source, onward, end, way in (
                        (t >= e, t - e, t - 1, t + 1, t < T - 1, 0), (t + e < T, t + e, t + 1, t - 1, t > 0, 1)):
                    @pl.when(here)
                    def _():
                        block = self.block(c, lat, tok)
                        arrived(block, self.chain_sem(c, d, tok), tok=tok if c in self.straight else source)
                        if e < T - 1 and c not in self.straight:
                            @pl.when(end)
                            def _():
                                self.move(block, block, self.sends.at[2 * self.kind(c) + way], self.chain_sem(c, d, tok), tok=onward)
                        if c not in self.ahead:
                            self.across(c, tok)

        def share(self, c, lat, slot):
            group = self.buf.at[c, lat]
            self.move(group, group, self.sends.at[6], self.lo.at[c, slot], lat=partner)

        def mine(self, c):
            self.share(c, a, 0)
            if c in self.ahead:
                for d in range(1, H):
                    self.share(c, self.other(d), d)

        def third(self, c):
            if c not in self.ahead:
                for d in range(1, H):
                    for tok in range(T):
                        arrived(self.block(c, self.other(d), tok), self.hi.at[c, d - 1, tok], lat=self.other(d))
                    self.share(c, self.other(d), d)

        def fourth(self, c):
            for d in range(H):
                arrived(self.buf.at[c, mod(h - d, H) * 2 + 1 - lo], self.lo.at[c, d], lat=partner)

        def finish(self):
            ahead, straight = len(self.ahead), len(self.straight)
            if straight and T > 1:
                sent(self.buf.at[pl.ds(0, straight), 0, pl.ds(0, T - 1)], self.sends.at[7], lat=partner)
                if H > 1:
                    sent(self.buf.at[pl.ds(0, straight), pl.ds(0, H - 1)], self.sends.at[4], lat=self.other(1))
            for kind, n, wide in ((0, self.count - ahead - straight, 1), (1, ahead, H)):
                if n == 0:
                    continue
                for m in range(1, T):
                    blocks = self.buf.at[pl.ds(0, n), pl.ds(0, wide), pl.ds(0, m)]

                    @pl.when(t + 1 == m)
                    def _():
                        sent(blocks, self.sends.at[2 * kind], tok=t + 1)

                    @pl.when(T - t == m)
                    def _():
                        sent(blocks, self.sends.at[2 * kind + 1], tok=t - 1)
                if H > 1:
                    sent(self.buf.at[pl.ds(0, n), pl.ds(0, H - 1), pl.ds(0, 1 if kind else T)], self.sends.at[4 + kind],
                         lat=self.other(1))
            sent(self.buf.at[:, pl.ds(0, H)], self.sends.at[6], lat=partner)

    straight = [c for c in range(C) if c >= C - STRAIGHT]
    gx, gs = Gather(xg, x_send, AHEAD_IN, [], B), Gather(sg, s_send, AHEAD, straight, C)
    recv_lo, recv_hi, recv_tok, recv_layer = rs_recv

    words_in = local_copy(words_ref.at[0], words_v, 2 * B + C)
    bias_in = local_copy(bias_ref, bias_v, 2 * B + C + 1)
    words_in.start()
    bias_in.start()
    enc_loads, dec_loads, own_loads = [], [], []
    for c in range(B):
        own_loads.append(local_copy(x_ref.at[0, :, cols(c, bw)], xg.at[c, a, t], c))
        enc_loads.append(local_copy(enc_ref.at[0, cols(c, bw), :], enc.at[c], B + c))
    for c in range(C):
        dec_loads.append(local_copy(dec_ref.at[0, :, cols(c)], dec.at[c], 2 * B + c))
    own_target = local_copy(t_ref.at[0], tg.at[l], 2 * B + C + 2)
    for copy in own_loads + enc_loads:
        copy.start()

    barrier = pltpu.get_barrier_semaphore()
    count = 0
    for name, index, n in (("tok", t, T), ("layer", l, L)):
        for d in range(1, n):
            pl.semaphore_signal(barrier, inc=1, device_id={name: mod(index + d, n)}, device_id_type=MESH)
            count += 1
    for d in range(1, H):
        pl.semaphore_signal(barrier, inc=1, device_id={"lat": mod(h + d, H) * 2 + lo}, device_id_type=MESH)
        count += 1
    pl.semaphore_signal(barrier, inc=1, device_id={"lat": partner}, device_id_type=MESH)
    pl.semaphore_wait(barrier, count + 1)

    for c in range(B):
        gx.first(c, x_ref.at[0, :, cols(c, bw)])
    for d in range(1, L):
        remote(t_ref.at[0], tg.at[l], tg_send, tg_recv.at[d - 1], layer=mod(l + d, L)).start()
    own_target.start()
    for copy in dec_loads:
        copy.start()

    W = words_v.shape[0]
    words_in.wait()
    bias_in.wait()
    words = words_v[...]
    low = (words & 255).astype(jnp.float32).astype(jnp.bfloat16)
    high = (jnp.right_shift(words, 8) & 255).astype(jnp.float32).astype(jnp.bfloat16)

    @pl.loop(0, F // TILE)
    def _(n):
        at = pl.ds(pl.multiple_of(n * TILE, TILE), TILE)
        col = lax.broadcasted_iota(jnp.int32, (W, TILE), 1) + n * TILE
        row = lax.broadcasted_iota(jnp.int32, (W, TILE), 0)
        same = jnp.right_shift(col, 4) == row
        first_byte = (col & 8) == 0
        spread_low = jnp.where(same & first_byte, 1.0, 0.0).astype(jnp.bfloat16)
        spread_high = jnp.where(same & jnp.logical_not(first_byte), 1.0, 0.0).astype(jnp.bfloat16)
        byte = (lax.dot_general(low, spread_low, (((0,), (0,)), ((), ())), preferred_element_type=jnp.float32)
                + lax.dot_general(high, spread_high, (((0,), (0,)), ((), ())), preferred_element_type=jnp.float32)).astype(jnp.int32)
        shift = lax.broadcasted_iota(jnp.int32, byte.shape, 1) & 7
        gate[:, at] = (jnp.right_shift(byte, shift) & 1).astype(jnp.float32)

    def matmul_in(c):
        enc_loads[c].wait()

        @pl.loop(0, F // TILE)
        def _(n):
            at = pl.ds(pl.multiple_of(n * TILE, TILE), TILE)
            part = jnp.dot(xg[c].reshape(N, bw), enc[c, :, at], preferred_element_type=jnp.float32)
            if c > 0:
                part = acc[:, at] + part
            if c < B - 1:
                acc[:, at] = part
            else:
                latent[:, at] = (gate[:, at] * (part + bias_v[:, at])).astype(jnp.bfloat16)

    for c in range(B):
        own_loads[c].wait()
    for c in gx.ahead:
        gx.cross(c)
    def hop_in(e):
        return lambda c: gx.hop(c, e)

    def last_in(c):
        gx.fourth(c)
        matmul_in(c)

    block = IN_PACE / B
    arrivals = [(hop_in(e), IN_PACE * e) for e in range(1, T)]
    arrivals += [(gx.mine, IN_PACE * (T - 1)), (gx.third, IN_PACE * (T - 1) + IN_LAG), (last_in, IN_PACE * (T - 1) + IN_LAST)]
    for _, i, c in sorted((begin + c * block, i, c) for i, (_, begin) in enumerate(arrivals) for c in range(B)):
        arrivals[i][0](c)

    def stage_matmul(c):
        dec_loads[c].wait()

        @pl.loop(0, cw // TILE)
        def _(n):
            at = pl.ds(pl.multiple_of(n * TILE, TILE), TILE)
            w[c, :, at] = jnp.dot(latent[...], dec[c, :, at], preferred_element_type=jnp.float32).astype(jnp.bfloat16)

        for k in range(H):
            to = mod(h + 1 + k, H)
            remote(w.at[c, group(to * 2 + 1 - lo), :], r1.at[c, to], rs_send.at[0], recv_lo.at[c, k], lat=partner).start()

    def stage_lo(c):
        for k in range(H):
            to = mod(h + 1 + k, H)
            arrived(r1.at[c, to], recv_lo.at[c, k], lat=partner)
            total = w[c, group(to * 2 + lo), :].astype(jnp.float32) + r1[c, to].astype(jnp.float32)
            if k < H - 1:
                s2[c, k] = total.astype(jnp.bfloat16)
                remote(s2.at[c, k], r2.at[c, k], rs_send.at[1], recv_hi.at[c, k], lat=to * 2 + lo).start()
            else:
                p2[c] = total

    def add_on(c, j, slot, source):
        arrived(r3.at[c, slot], recv_tok.at[c, slot], tok=source)
        p2[c, j * r:(j + 1) * r] = p2[c, j * r:(j + 1) * r] + r3[c, slot].astype(jnp.float32)

    def pass_on(c, j, to, slot):
        s3[c, j] = p2[c, j * r:(j + 1) * r].astype(jnp.bfloat16)
        remote(s3.at[c, j], r3.at[c, slot], rs_send.at[2], recv_tok.at[c, slot], tok=to).start()

    def stage_hi(c):
        total = p2[c]
        for k in range(H - 1):
            arrived(r2.at[c, k], recv_hi.at[c, k], lat=mod(h - 1 - k, H) * 2 + lo)
            total = total + r2[c, k].astype(jnp.float32)
        p2[c] = total
        if c >= C - STRAIGHT_SUMS:
            for j in range(T):
                s3[c, j] = total[j * r:(j + 1) * r].astype(jnp.bfloat16)
            for d in range(T - 1, 0, -1):
                to = mod(t + d, T)
                remote(s3.at[c, to], r3.at[c, t], rs_send.at[2], recv_tok.at[c, t], tok=to).start()
        elif T > 1:
            chain(0)(c)

    def chain(e):
        def run(c):
            @pl.when(t == e)
            def _():
                for j in range(T - 1, e, -1):
                    if e > 0:
                        add_on(c, j, j, e - 1)
                    pass_on(c, j, e + 1, j)
                if e > 0:
                    add_on(c, e, e, e - 1)

            @pl.when(t == T - 1 - e)
            def _():
                q = T - 1 - e
                for j in range(q):
                    if e > 0:
                        add_on(c, j, j, q + 1)
                    pass_on(c, j, q - 1, T if j == q - 1 else j)
                if e > 0:
                    add_on(c, q, T, q + 1)
        return run

    def stage_tok(c):
        total = p2[c, pl.ds(pl.multiple_of(t * r, 8), r)]
        if c >= C - STRAIGHT_SUMS:
            for d in range(1, T):
                source = mod(t - d, T)
                arrived(r3.at[c, source], recv_tok.at[c, source], tok=source)
                total = total + r3[c, source].astype(jnp.float32)
        w4[c, l] = total.astype(jnp.bfloat16)
        for d in range(1, L):
            remote(w4.at[c, l], w4.at[c, l], rs_send.at[3], recv_layer.at[c, d - 1], layer=mod(l + d, L)).start()

    diff_out = local_copy(diff_v, diff_ref, 2 * B + C + 3)

    def stage_layer(c):
        if c == 0:
            own_target.wait()
            for d in range(1, L):
                arrived(tg.at[mod(l - d, L)], tg_recv.at[d - 1], layer=mod(l - d, L))
        for d in range(1, L):
            arrived(w4.at[c, mod(l - d, L)], recv_layer.at[c, d - 1], layer=mod(l - d, L))
        running = jnp.zeros((r, cw), jnp.float32)
        later = jnp.zeros((r, cw), jnp.float32)
        mine = jnp.zeros((r, cw), jnp.float32)
        for i in range(L):
            running = running + w4[c, i].astype(jnp.float32)
            difference = running - tg[i, :, cols(c)].astype(jnp.float32)
            mine = mine + difference * (l == i).astype(jnp.float32)
            later = later + difference * (l <= i).astype(jnp.float32)
        sg[c, a, t] = later.astype(jnp.bfloat16)
        gs.first(c)
        diff_v[:, cols(c)] = mine.astype(jnp.bfloat16)
        if c == C - 1:
            diff_out.start()

    def stage_cross(c):
        if c in gs.ahead:
            gs.cross(c)

    def stage_hop(e):
        def run(c):
            gs.hop(c, e)
        return run

    def stage_out(c):
        gs.fourth(c)
        local_copy(sg.at[c], sig_ref.at[c], 2 * B + C + 4).start()

    lat_out = local_copy(turned, lat_ref, 2 * B + C + 5)

    def turn():
        @pl.loop(0, F // TILE)
        def _(n):
            at = pl.ds(pl.multiple_of(n * TILE, TILE), TILE)
            turned[at, :] = latent[:, at].astype(jnp.float32).T.astype(jnp.bfloat16)

        lat_out.start()

    pace = PACE / C
    plan = []
    for c in range(C):
        near, far = c >= C - STRAIGHT_SUMS, c in straight
        plan += [(c * MXU / C, stage_matmul, c), ((c + 1) * MXU / C + 0.5, stage_lo, c)]
        at = HEAD + pace * (c + 1)
        plan += [(at, stage_hi, c)]
        if not near:
            plan += [(at + LINK * e, chain(e), c) for e in range(1, T)]
        at += 4.0 if near else LINK * (T - 1) + 0.2
        plan += [(at, stage_tok, c), (at + NEXT, stage_layer, c), (at + NEXT + 2.5, stage_cross, c)]
        plan += [(at + NEXT + (2.0 + 0.5 * e if far else HOP * e), stage_hop(e), c) for e in range(1, T)]
        at += NEXT + (2.0 + 0.5 * (T - 1) if far else HOP * (T - 1))
        plan += [(at, gs.mine, c), (at + 2.5, gs.third, c), (at + 4.0, stage_out, c)]
    turned_yet = False
    for when, stage, c in sorted(plan, key=lambda p: p[0]):
        if when > MXU + 2.0 and not turned_yet:
            turn()
            turned_yet = True
        stage(c)

    local_copy(sg, sig_ref, 2 * B + C + 4).wait()
    diff_out.wait()
    lat_out.wait()
    gx.finish()
    gs.finish()
    sent(r1, rs_send.at[0], lat=partner)
    if H > 1:
        sent(r2, rs_send.at[1], lat=gs.other(1))
    if T > 1:
        sent(s3.at[:, pl.ds(0, T - 1)], rs_send.at[2], tok=mod(t + 1, T))
    if L > 1:
        sent(w4.at[:, pl.ds(0, L - 1)], rs_send.at[3], layer=mod(l + 1, L))
        sent(tg.at[pl.ds(0, L - 1)], tg_send, layer=mod(l + 1, L))


def product(lat_ref, sig_ref, diff_ref, out_diff_ref, grad_ref, lat, sig, diff, grad, in_sems, out_sems):
    C, N, cw = sig_ref.shape
    loads = [pltpu.make_async_copy(sig_ref.at[c], sig.at[c], in_sems.at[c]) for c in range(C)]
    lat_in = pltpu.make_async_copy(lat_ref, lat, in_sems.at[C])
    diff_in = pltpu.make_async_copy(diff_ref, diff, in_sems.at[C + 1])
    outs = [pltpu.make_async_copy(grad.at[c], grad_ref.at[0, :, pl.ds(c * cw, cw)], out_sems.at[c]) for c in range(C)]
    outs.append(pltpu.make_async_copy(diff, out_diff_ref.at[0], out_sems.at[C]))
    for copy in (lat_in, *loads, diff_in):
        copy.start()
    lat_in.wait()
    for c in range(C):
        loads[c].wait()
        for n in range(0, cw, TILE):
            total = jnp.dot(lat[...], sig[c, :, n:n + TILE], preferred_element_type=jnp.float32)
            grad[c, :, n:n + TILE] = (total * (1.0 / N)).astype(jnp.bfloat16)
        outs[c].start()
    diff_in.wait()
    outs[C].start()
    for copy in outs:
        copy.wait()


def gradient(latent, signal, difference):
    F, N = latent.shape
    C, _, cw = signal.shape
    r, D = difference.shape
    bf = jnp.bfloat16
    hbm = pl.BlockSpec(memory_space=pl.ANY)
    return pl.pallas_call(
        product,
        in_specs=[hbm, hbm, hbm],
        out_specs=(hbm, hbm),
        out_shape=(jax.ShapeDtypeStruct((1, r, D), bf), jax.ShapeDtypeStruct((1, F, D), bf)),
        scratch_shapes=[
            pltpu.VMEM((F, N), bf),
            pltpu.VMEM((C, N, cw), bf),
            pltpu.VMEM((r, D), bf),
            pltpu.VMEM((C, F, cw), bf),
            pltpu.SemaphoreType.DMA((C + 2,)),
            pltpu.SemaphoreType.DMA((C + 1,)),
        ],
        compiler_params=pltpu.CompilerParams(vmem_limit_bytes=60 * 1024 * 1024),
    )(latent, signal, difference)


def fused(mesh, mlp_inputs, mlp_outputs, encoder, encoder_bias, active_words, decoder):
    L, A, T = mesh.shape["layer"], mesh.shape["lat"], mesh.shape["tok"]
    _, r, D = mlp_inputs.shape
    F = encoder.shape[2]
    N, W = active_words.shape[1:]
    B, C, H, depth = IN_CHUNKS, CHUNKS, A // 2, T * r
    bw, cw, most = D // B, D // C, max(IN_CHUNKS, CHUNKS)
    bf, f32 = jnp.bfloat16, jnp.float32
    hbm = pl.BlockSpec(memory_space=pl.ANY)

    def dma(*shape):
        return pltpu.SemaphoreType.DMA(tuple(max(n, 1) for n in shape))

    return pl.pallas_call(
        functools.partial(kernel, (L, A, T, r, B, C, F)),
        out_shape=(jax.ShapeDtypeStruct((r, D), bf), jax.ShapeDtypeStruct((C, A, T, r, cw), bf), jax.ShapeDtypeStruct((F, N), bf)),
        in_specs=[hbm] * 6,
        out_specs=(hbm, hbm, hbm),
        scratch_shapes=[
            pltpu.VMEM((B, A, T, r, bw), bf),
            pltpu.VMEM((C, A, T, r, cw), bf),
            pltpu.VMEM((B, bw, F), bf),
            pltpu.VMEM((C, F, cw), bf),
            pltpu.VMEM((N, F), f32),
            pltpu.VMEM((N, F), f32),
            pltpu.VMEM((N, F), bf),
            pltpu.VMEM((F, N), bf),
            pltpu.VMEM((C, N, cw), bf),
            pltpu.VMEM((C, H, depth, cw), bf),
            pltpu.VMEM((C, max(H - 1, 1), depth, cw), bf),
            pltpu.VMEM((C, depth, cw), f32),
            pltpu.VMEM((C, max(H - 1, 1), depth, cw), bf),
            pltpu.VMEM((C, T, r, cw), bf),
            pltpu.VMEM((C, T + 1, r, cw), bf),
            pltpu.VMEM((C, L, r, cw), bf),
            pltpu.VMEM((L, r, D), bf),
            pltpu.VMEM((W, N), jnp.int32),
            pltpu.VMEM((1, F), f32),
            pltpu.VMEM((r, D), bf),
            [dma(most, T), dma(max(len(AHEAD_IN), len(AHEAD)), H - 1, T), dma(most, H - 1, T), dma(most, H)],
            dma(8),
            dma(8),
            dma(4),
            [dma(C, H), dma(C, H - 1), dma(C, T + 1), dma(C, L - 1)],
            pltpu.SemaphoreType.DMA,
            dma(L - 1),
            dma(2 * B + C + 6),
        ],
        compiler_params=pltpu.CompilerParams(
            collective_id=0, has_side_effects=True, vmem_limit_bytes=60 * 1024 * 1024),
    )(mlp_inputs, mlp_outputs, encoder, encoder_bias, jnp.transpose(active_words, (0, 2, 1)), decoder)


def local(mesh, mlp_inputs, mlp_outputs, encoder, encoder_bias, active_words, decoder):
    difference, signal, latent = fused(mesh, mlp_inputs, mlp_outputs, encoder, encoder_bias, active_words, decoder)
    return gradient(latent, signal.reshape(signal.shape[0], latent.shape[1], signal.shape[-1]), difference)


def solution(mesh):
    in_specs = (
        P("layer", ("lat", "tok"), None),
        P("layer", ("lat", "tok"), None),
        P("layer", None, ("lat", "tok")),
        P("layer", ("lat", "tok")),
        P("layer", None, ("lat", "tok")),
        P("layer", ("lat", "tok"), None),
    )
    out_specs = (P("layer", ("lat", "tok"), None), P("layer", ("lat", "tok"), None))
    return jax.shard_map(functools.partial(local, mesh), mesh=mesh, in_specs=in_specs, out_specs=out_specs, check_vma=False)
```

```python
import functools

import jax
import jax.numpy as jnp
from jax import lax
from jax.experimental import pallas as pl
from jax.experimental.pallas import tpu as pltpu
from jax.sharding import PartitionSpec as P

MESH = pl.DeviceIdType.MESH
IN_CHUNKS = 4
CHUNKS = 8
AHEAD_IN = ()
AHEAD = ()
TILE = 512
IN_PACE = 4.3
PACE = 11.0
MXU = 6.0
HOP = 3.0
LINK = 2.3
HEAD = 4.0
NEXT = 2.0
IN_LAG = 2.6
IN_LAST = 4.2
STRAIGHT = 4
STRAIGHT_SUMS = 0


def kernel(sizes, x_ref, t_ref, enc_ref, bias_ref, words_ref, dec_ref,
           diff_ref, sig_ref, lat_ref,
           xg, sg, enc, dec, acc, gate, latent, turned, w, r1, s2, p2, r2, s3, r3, w4, tg, words_v, bias_v, diff_v,
           gather_recv, x_send, s_send, rs_send, rs_recv, tg_send, tg_recv, loc_sems):
    L, A, T, r, B, C, F = sizes
    D = x_ref.shape[2]
    bw, cw = D // B, D // C
    H = A // 2
    N = A * T * r
    depth = T * r
    l, a, t = lax.axis_index("layer"), lax.axis_index("lat"), lax.axis_index("tok")
    h, lo = a // 2, lax.rem(a, 2)
    partner = h * 2 + 1 - lo

    def mod(v, n):
        return lax.rem(v + n, n)

    def group(lat):
        return pl.ds(pl.multiple_of(lat * depth, 8), depth)

    def cols(c, wide=cw):
        return pl.ds(c * wide, wide)

    def remote(src, dst, send_sem, recv_sem, **where):
        return pltpu.make_async_remote_copy(
            src_ref=src, dst_ref=dst, send_sem=send_sem, recv_sem=recv_sem, device_id=where, device_id_type=MESH)

    def arrived(dst, sem, **where):
        remote(dst, dst, sem, sem, **where).wait_recv()

    def sent(ref, sem, **where):
        remote(ref, ref, sem, sem, **where).wait_send()

    def local_copy(src, dst, at):
        return pltpu.make_async_copy(src, dst, loc_sems.at[at])

    class Gather:
        def __init__(self, buf, sends, ahead, straight, count):
            self.straight = straight
            self.buf, self.ahead, self.count = buf, [c for c in ahead if c < count and H > 1], count
            self.chain, self.others, self.hi, self.lo = gather_recv
            self.sends = sends

        def block(self, c, lat, tok):
            return self.buf.at[c, lat, tok]

        def kind(self, c):
            return 1 if c in self.ahead else 0

        def other(self, d):
            return mod(h - d, H) * 2 + lo

        def chain_sem(self, c, d, tok):
            return self.chain.at[c, tok] if d == 0 else self.others.at[self.ahead.index(c), d - 1, tok]

        def move(self, src, dst, send_sem, recv_sem, **where):
            remote(src, dst, send_sem, recv_sem, **where).start()

        def along(self, c, d, src=None):
            lat = a if d == 0 else self.other(d)
            block = self.block(c, lat, t)

            @pl.when(t < T - 1)
            def _():
                self.move(src or block, block, self.sends.at[2 * self.kind(c)], self.chain_sem(c, d, t), tok=t + 1)

            @pl.when(t > 0)
            def _():
                self.move(src or block, block, self.sends.at[2 * self.kind(c) + 1], self.chain_sem(c, d, t), tok=t - 1)

        def across(self, c, tok, src=None):
            block = self.block(c, a, tok)
            for d in range(1, H):
                self.move(src or block, block, self.sends.at[4 + self.kind(c)], self.hi.at[c, d - 1], lat=mod(h + d, H) * 2 + lo)

        def first(self, c, src=None):
            if c in self.ahead:
                self.across(c, t, src)
                self.along(c, 0, src)
            elif c in self.straight:
                block = self.block(c, a, t)
                for e in range(T - 1, 0, -1):
                    for fits, to in ((t + e < T, t + e), (t >= e, t - e)):
                        @pl.when(fits)
                        def _():
                            self.move(src or block, block, self.sends.at[7], self.chain_sem(c, 0, t), tok=to)
                self.across(c, t, src)
            else:
                self.along(c, 0, src)
                self.across(c, t, src)

        def cross(self, c):
            for d in range(1, H):
                arrived(self.block(c, self.other(d), t), self.hi.at[c, d - 1], lat=self.other(d))
                self.along(c, d)

        def hop(self, c, e):
            for d in range(H if c in self.ahead else 1):
                lat = a if d == 0 else self.other(d)
                for here, tok, source, onward, end, way in (
                        (t >= e, t - e, t - 1, t + 1, t < T - 1, 0), (t + e < T, t + e, t + 1, t - 1, t > 0, 1)):
                    @pl.when(here)
                    def _():
                        block = self.block(c, lat, tok)
                        arrived(block, self.chain_sem(c, d, tok), tok=tok if c in self.straight else source)
                        if e < T - 1 and c not in self.straight:
                            @pl.when(end)
                            def _():
                                self.move(block, block, self.sends.at[2 * self.kind(c) + way], self.chain_sem(c, d, tok), tok=onward)
                        if c not in self.ahead:
                            self.across(c, tok)

        def share(self, c, lat, slot):
            group = self.buf.at[c, lat]
            self.move(group, group, self.sends.at[6], self.lo.at[c, slot], lat=partner)

        def mine(self, c):
            self.share(c, a, 0)
            if c in self.ahead:
                for d in range(1, H):
                    self.share(c, self.other(d), d)

        def third(self, c):
            if c not in self.ahead:
                for d in range(1, H):
                    arrived(self.buf.at[c, self.other(d)], self.hi.at[c, d - 1], lat=self.other(d))
                    self.share(c, self.other(d), d)

        def fourth(self, c):
            for d in range(H):
                arrived(self.buf.at[c, mod(h - d, H) * 2 + 1 - lo], self.lo.at[c, d], lat=partner)

        def finish(self):
            ahead, straight = len(self.ahead), len(self.straight)
            if straight and T > 1:
                sent(self.buf.at[pl.ds(0, straight), 0, pl.ds(0, T - 1)], self.sends.at[7], lat=partner)
                if H > 1:
                    sent(self.buf.at[pl.ds(0, straight), pl.ds(0, H - 1)], self.sends.at[4], lat=self.other(1))
            for kind, n, wide in ((0, self.count - ahead - straight, 1), (1, ahead, H)):
                if n == 0:
                    continue
                for m in range(1, T):
                    blocks = self.buf.at[pl.ds(0, n), pl.ds(0, wide), pl.ds(0, m)]

                    @pl.when(t + 1 == m)
                    def _():
                        sent(blocks, self.sends.at[2 * kind], tok=t + 1)

                    @pl.when(T - t == m)
                    def _():
                        sent(blocks, self.sends.at[2 * kind + 1], tok=t - 1)
                if H > 1:
                    sent(self.buf.at[pl.ds(0, n), pl.ds(0, H - 1), pl.ds(0, 1 if kind else T)], self.sends.at[4 + kind],
                         lat=self.other(1))
            sent(self.buf.at[:, pl.ds(0, H)], self.sends.at[6], lat=partner)

    straight = [c for c in range(C) if c >= C - STRAIGHT]
    gx, gs = Gather(xg, x_send, AHEAD_IN, [], B), Gather(sg, s_send, AHEAD, straight, C)
    recv_lo, recv_hi, recv_tok, recv_layer = rs_recv

    words_in = local_copy(words_ref.at[0], words_v, 2 * B + C)
    bias_in = local_copy(bias_ref, bias_v, 2 * B + C + 1)
    words_in.start()
    bias_in.start()
    enc_loads, dec_loads, own_loads = [], [], []
    for c in range(B):
        own_loads.append(local_copy(x_ref.at[0, :, cols(c, bw)], xg.at[c, a, t], c))
        enc_loads.append(local_copy(enc_ref.at[0, cols(c, bw), :], enc.at[c], B + c))
    for c in range(C):
        dec_loads.append(local_copy(dec_ref.at[0, :, cols(c)], dec.at[c], 2 * B + c))
    own_target = local_copy(t_ref.at[0], tg.at[l], 2 * B + C + 2)
    for copy in own_loads + enc_loads:
        copy.start()

    barrier = pltpu.get_barrier_semaphore()
    count = 0
    for name, index, n in (("tok", t, T), ("layer", l, L)):
        for d in range(1, n):
            pl.semaphore_signal(barrier, inc=1, device_id={name: mod(index + d, n)}, device_id_type=MESH)
            count += 1
    for d in range(1, H):
        pl.semaphore_signal(barrier, inc=1, device_id={"lat": mod(h + d, H) * 2 + lo}, device_id_type=MESH)
        count += 1
    pl.semaphore_signal(barrier, inc=1, device_id={"lat": partner}, device_id_type=MESH)
    pl.semaphore_wait(barrier, count + 1)

    for c in range(B):
        gx.first(c, x_ref.at[0, :, cols(c, bw)])
    for d in range(1, L):
        remote(t_ref.at[0], tg.at[l], tg_send, tg_recv.at[d - 1], layer=mod(l + d, L)).start()
    own_target.start()
    for copy in dec_loads:
        copy.start()

    W = words_v.shape[0]
    words_in.wait()
    bias_in.wait()
    words = words_v[...]
    low = (words & 255).astype(jnp.float32).astype(jnp.bfloat16)
    high = (jnp.right_shift(words, 8) & 255).astype(jnp.float32).astype(jnp.bfloat16)

    @pl.loop(0, F // TILE)
    def _(n):
        at = pl.ds(pl.multiple_of(n * TILE, TILE), TILE)
        col = lax.broadcasted_iota(jnp.int32, (W, TILE), 1) + n * TILE
        row = lax.broadcasted_iota(jnp.int32, (W, TILE), 0)
        same = jnp.right_shift(col, 4) == row
        first_byte = (col & 8) == 0
        spread_low = jnp.where(same & first_byte, 1.0, 0.0).astype(jnp.bfloat16)
        spread_high = jnp.where(same & jnp.logical_not(first_byte), 1.0, 0.0).astype(jnp.bfloat16)
        byte = (lax.dot_general(low, spread_low, (((0,), (0,)), ((), ())), preferred_element_type=jnp.float32)
                + lax.dot_general(high, spread_high, (((0,), (0,)), ((), ())), preferred_element_type=jnp.float32)).astype(jnp.int32)
        shift = lax.broadcasted_iota(jnp.int32, byte.shape, 1) & 7
        gate[:, at] = (jnp.right_shift(byte, shift) & 1).astype(jnp.float32)

    def matmul_in(c):
        enc_loads[c].wait()

        @pl.loop(0, F // TILE)
        def _(n):
            at = pl.ds(pl.multiple_of(n * TILE, TILE), TILE)
            part = jnp.dot(xg[c].reshape(N, bw), enc[c, :, at], preferred_element_type=jnp.float32)
            if c > 0:
                part = acc[:, at] + part
            if c < B - 1:
                acc[:, at] = part
            else:
                latent[:, at] = (gate[:, at] * (part + bias_v[:, at])).astype(jnp.bfloat16)

    for c in range(B):
        own_loads[c].wait()
    for c in gx.ahead:
        gx.cross(c)
    def hop_in(e):
        return lambda c: gx.hop(c, e)

    def last_in(c):
        gx.fourth(c)
        matmul_in(c)

    block = IN_PACE / B
    arrivals = [(hop_in(e), IN_PACE * e) for e in range(1, T)]
    arrivals += [(gx.mine, IN_PACE * (T - 1)), (gx.third, IN_PACE * (T - 1) + IN_LAG), (last_in, IN_PACE * (T - 1) + IN_LAST)]
    for _, i, c in sorted((begin + c * block, i, c) for i, (_, begin) in enumerate(arrivals) for c in range(B)):
        arrivals[i][0](c)

    def stage_matmul(c):
        dec_loads[c].wait()

        @pl.loop(0, cw // TILE)
        def _(n):
            at = pl.ds(pl.multiple_of(n * TILE, TILE), TILE)
            w[c, :, at] = jnp.dot(latent[...], dec[c, :, at], preferred_element_type=jnp.float32).astype(jnp.bfloat16)

        for k in range(H):
            to = mod(h + 1 + k, H)
            remote(w.at[c, group(to * 2 + 1 - lo), :], r1.at[c, to], rs_send.at[0], recv_lo.at[c, k], lat=partner).start()

    def stage_lo(c):
        for k in range(H):
            to = mod(h + 1 + k, H)
            arrived(r1.at[c, to], recv_lo.at[c, k], lat=partner)
            total = w[c, group(to * 2 + lo), :].astype(jnp.float32) + r1[c, to].astype(jnp.float32)
            if k < H - 1:
                s2[c, k] = total.astype(jnp.bfloat16)
                remote(s2.at[c, k], r2.at[c, k], rs_send.at[1], recv_hi.at[c, k], lat=to * 2 + lo).start()
            else:
                p2[c] = total

    def add_on(c, j, slot, source):
        arrived(r3.at[c, slot], recv_tok.at[c, slot], tok=source)
        p2[c, j * r:(j + 1) * r] = p2[c, j * r:(j + 1) * r] + r3[c, slot].astype(jnp.float32)

    def pass_on(c, j, to, slot):
        s3[c, j] = p2[c, j * r:(j + 1) * r].astype(jnp.bfloat16)
        remote(s3.at[c, j], r3.at[c, slot], rs_send.at[2], recv_tok.at[c, slot], tok=to).start()

    def stage_hi(c):
        total = p2[c]
        for k in range(H - 1):
            arrived(r2.at[c, k], recv_hi.at[c, k], lat=mod(h - 1 - k, H) * 2 + lo)
            total = total + r2[c, k].astype(jnp.float32)
        p2[c] = total
        if c >= C - STRAIGHT_SUMS:
            for j in range(T):
                s3[c, j] = total[j * r:(j + 1) * r].astype(jnp.bfloat16)
            for d in range(T - 1, 0, -1):
                to = mod(t + d, T)
                remote(s3.at[c, to], r3.at[c, t], rs_send.at[2], recv_tok.at[c, t], tok=to).start()
        elif T > 1:
            chain(0)(c)

    def chain(e):
        def run(c):
            @pl.when(t == e)
            def _():
                for j in range(T - 1, e, -1):
                    if e > 0:
                        add_on(c, j, j, e - 1)
                    pass_on(c, j, e + 1, j)
                if e > 0:
                    add_on(c, e, e, e - 1)

            @pl.when(t == T - 1 - e)
            def _():
                q = T - 1 - e
                for j in range(q):
                    if e > 0:
                        add_on(c, j, j, q + 1)
                    pass_on(c, j, q - 1, T if j == q - 1 else j)
                if e > 0:
                    add_on(c, q, T, q + 1)
        return run

    def stage_tok(c):
        total = p2[c, pl.ds(pl.multiple_of(t * r, 8), r)]
        if c >= C - STRAIGHT_SUMS:
            for d in range(1, T):
                source = mod(t - d, T)
                arrived(r3.at[c, source], recv_tok.at[c, source], tok=source)
                total = total + r3[c, source].astype(jnp.float32)
        w4[c, l] = total.astype(jnp.bfloat16)
        for d in range(1, L):
            remote(w4.at[c, l], w4.at[c, l], rs_send.at[3], recv_layer.at[c, d - 1], layer=mod(l + d, L)).start()

    diff_out = local_copy(diff_v, diff_ref, 2 * B + C + 3)

    def stage_layer(c):
        if c == 0:
            own_target.wait()
            for d in range(1, L):
                arrived(tg.at[mod(l - d, L)], tg_recv.at[d - 1], layer=mod(l - d, L))
        for d in range(1, L):
            arrived(w4.at[c, mod(l - d, L)], recv_layer.at[c, d - 1], layer=mod(l - d, L))
        running = jnp.zeros((r, cw), jnp.float32)
        later = jnp.zeros((r, cw), jnp.float32)
        mine = jnp.zeros((r, cw), jnp.float32)
        for i in range(L):
            running = running + w4[c, i].astype(jnp.float32)
            difference = running - tg[i, :, cols(c)].astype(jnp.float32)
            mine = mine + difference * (l == i).astype(jnp.float32)
            later = later + difference * (l <= i).astype(jnp.float32)
        sg[c, a, t] = later.astype(jnp.bfloat16)
        gs.first(c)
        diff_v[:, cols(c)] = mine.astype(jnp.bfloat16)
        if c == C - 1:
            diff_out.start()

    def stage_cross(c):
        if c in gs.ahead:
            gs.cross(c)

    def stage_hop(e):
        def run(c):
            gs.hop(c, e)
        return run

    def stage_out(c):
        gs.fourth(c)
        local_copy(sg.at[c], sig_ref.at[c], 2 * B + C + 4).start()

    lat_out = local_copy(turned, lat_ref, 2 * B + C + 5)

    def turn():
        @pl.loop(0, F // TILE)
        def _(n):
            at = pl.ds(pl.multiple_of(n * TILE, TILE), TILE)
            turned[at, :] = latent[:, at].astype(jnp.float32).T.astype(jnp.bfloat16)

        lat_out.start()

    pace = PACE / C
    plan = []
    for c in range(C):
        near, far = c >= C - STRAIGHT_SUMS, c in straight
        plan += [(c * MXU / C, stage_matmul, c), ((c + 1) * MXU / C + 0.5, stage_lo, c)]
        at = HEAD + pace * (c + 1)
        plan += [(at, stage_hi, c)]
        if not near:
            plan += [(at + LINK * e, chain(e), c) for e in range(1, T)]
        at += 4.0 if near else LINK * (T - 1) + 0.2
        plan += [(at, stage_tok, c), (at + NEXT, stage_layer, c), (at + NEXT + 2.5, stage_cross, c)]
        plan += [(at + NEXT + (2.0 + 0.5 * e if far else HOP * e), stage_hop(e), c) for e in range(1, T)]
        at += NEXT + (2.0 + 0.5 * (T - 1) if far else HOP * (T - 1))
        plan += [(at, gs.mine, c), (at + 2.5, gs.third, c), (at + 4.0, stage_out, c)]
    turned_yet = False
    for when, stage, c in sorted(plan, key=lambda p: p[0]):
        if when > MXU + 2.0 and not turned_yet:
            turn()
            turned_yet = True
        stage(c)

    local_copy(sg, sig_ref, 2 * B + C + 4).wait()
    diff_out.wait()
    lat_out.wait()
    gx.finish()
    gs.finish()
    sent(r1, rs_send.at[0], lat=partner)
    if H > 1:
        sent(r2, rs_send.at[1], lat=gs.other(1))
    if T > 1:
        sent(s3.at[:, pl.ds(0, T - 1)], rs_send.at[2], tok=mod(t + 1, T))
    if L > 1:
        sent(w4.at[:, pl.ds(0, L - 1)], rs_send.at[3], layer=mod(l + 1, L))
        sent(tg.at[pl.ds(0, L - 1)], tg_send, layer=mod(l + 1, L))


def product(lat_ref, sig_ref, diff_ref, out_diff_ref, grad_ref, lat, sig, diff, grad, in_sems, out_sems):
    C, N, cw = sig_ref.shape
    loads = [pltpu.make_async_copy(sig_ref.at[c], sig.at[c], in_sems.at[c]) for c in range(C)]
    lat_in = pltpu.make_async_copy(lat_ref, lat, in_sems.at[C])
    diff_in = pltpu.make_async_copy(diff_ref, diff, in_sems.at[C + 1])
    outs = [pltpu.make_async_copy(grad.at[c], grad_ref.at[0, :, pl.ds(c * cw, cw)], out_sems.at[c]) for c in range(C)]
    outs.append(pltpu.make_async_copy(diff, out_diff_ref.at[0], out_sems.at[C]))
    for copy in (lat_in, *loads, diff_in):
        copy.start()
    lat_in.wait()
    for c in range(C):
        loads[c].wait()
        for n in range(0, cw, TILE):
            total = jnp.dot(lat[...], sig[c, :, n:n + TILE], preferred_element_type=jnp.float32)
            grad[c, :, n:n + TILE] = (total * (1.0 / N)).astype(jnp.bfloat16)
        outs[c].start()
    diff_in.wait()
    outs[C].start()
    for copy in outs:
        copy.wait()


def gradient(latent, signal, difference):
    F, N = latent.shape
    C, _, cw = signal.shape
    r, D = difference.shape
    bf = jnp.bfloat16
    hbm = pl.BlockSpec(memory_space=pl.ANY)
    return pl.pallas_call(
        product,
        in_specs=[hbm, hbm, hbm],
        out_specs=(hbm, hbm),
        out_shape=(jax.ShapeDtypeStruct((1, r, D), bf), jax.ShapeDtypeStruct((1, F, D), bf)),
        scratch_shapes=[
            pltpu.VMEM((F, N), bf),
            pltpu.VMEM((C, N, cw), bf),
            pltpu.VMEM((r, D), bf),
            pltpu.VMEM((C, F, cw), bf),
            pltpu.SemaphoreType.DMA((C + 2,)),
            pltpu.SemaphoreType.DMA((C + 1,)),
        ],
        compiler_params=pltpu.CompilerParams(vmem_limit_bytes=60 * 1024 * 1024),
    )(latent, signal, difference)


def fused(mesh, mlp_inputs, mlp_outputs, encoder, encoder_bias, active_words, decoder):
    L, A, T = mesh.shape["layer"], mesh.shape["lat"], mesh.shape["tok"]
    _, r, D = mlp_inputs.shape
    F = encoder.shape[2]
    N, W = active_words.shape[1:]
    B, C, H, depth = IN_CHUNKS, CHUNKS, A // 2, T * r
    bw, cw, most = D // B, D // C, max(IN_CHUNKS, CHUNKS)
    bf, f32 = jnp.bfloat16, jnp.float32
    hbm = pl.BlockSpec(memory_space=pl.ANY)

    def dma(*shape):
        return pltpu.SemaphoreType.DMA(tuple(max(n, 1) for n in shape))

    return pl.pallas_call(
        functools.partial(kernel, (L, A, T, r, B, C, F)),
        out_shape=(jax.ShapeDtypeStruct((r, D), bf), jax.ShapeDtypeStruct((C, A, T, r, cw), bf), jax.ShapeDtypeStruct((F, N), bf)),
        in_specs=[hbm] * 6,
        out_specs=(hbm, hbm, hbm),
        scratch_shapes=[
            pltpu.VMEM((B, A, T, r, bw), bf),
            pltpu.VMEM((C, A, T, r, cw), bf),
            pltpu.VMEM((B, bw, F), bf),
            pltpu.VMEM((C, F, cw), bf),
            pltpu.VMEM((N, F), f32),
            pltpu.VMEM((N, F), f32),
            pltpu.VMEM((N, F), bf),
            pltpu.VMEM((F, N), bf),
            pltpu.VMEM((C, N, cw), bf),
            pltpu.VMEM((C, H, depth, cw), bf),
            pltpu.VMEM((C, max(H - 1, 1), depth, cw), bf),
            pltpu.VMEM((C, depth, cw), f32),
            pltpu.VMEM((C, max(H - 1, 1), depth, cw), bf),
            pltpu.VMEM((C, T, r, cw), bf),
            pltpu.VMEM((C, T + 1, r, cw), bf),
            pltpu.VMEM((C, L, r, cw), bf),
            pltpu.VMEM((L, r, D), bf),
            pltpu.VMEM((W, N), jnp.int32),
            pltpu.VMEM((1, F), f32),
            pltpu.VMEM((r, D), bf),
            [dma(most, T), dma(max(len(AHEAD_IN), len(AHEAD)), H - 1, T), dma(most, H - 1), dma(most, H)],
            dma(8),
            dma(8),
            dma(4),
            [dma(C, H), dma(C, H - 1), dma(C, T + 1), dma(C, L - 1)],
            pltpu.SemaphoreType.DMA,
            dma(L - 1),
            dma(2 * B + C + 6),
        ],
        compiler_params=pltpu.CompilerParams(
            collective_id=0, has_side_effects=True, vmem_limit_bytes=60 * 1024 * 1024),
    )(mlp_inputs, mlp_outputs, encoder, encoder_bias, jnp.transpose(active_words, (0, 2, 1)), decoder)


def local(mesh, mlp_inputs, mlp_outputs, encoder, encoder_bias, active_words, decoder):
    difference, signal, latent = fused(mesh, mlp_inputs, mlp_outputs, encoder, encoder_bias, active_words, decoder)
    return gradient(latent, signal.reshape(signal.shape[0], latent.shape[1], signal.shape[-1]), difference)


def solution(mesh):
    in_specs = (
        P("layer", ("lat", "tok"), None),
        P("layer", ("lat", "tok"), None),
        P("layer", None, ("lat", "tok")),
        P("layer", ("lat", "tok")),
        P("layer", None, ("lat", "tok")),
        P("layer", ("lat", "tok"), None),
    )
    out_specs = (P("layer", ("lat", "tok"), None), P("layer", ("lat", "tok"), None))
    return jax.shard_map(functools.partial(local, mesh), mesh=mesh, in_specs=in_specs, out_specs=out_specs, check_vma=False)
```
